256 devices in a mesh: lon: 16 (over z, x_hi), lat: 16 (over y, x_lo, core).
Axes of the slice: x: 4 (x_hi: 2, x_lo: 2; x = x_hi * 2 + x_lo), y: 4, z: 8, core: 2. Of those that a mesh axis runs over, the one named last changes fastest.
Arguments:
- features: bfloat16 [720, 720, 192], P('lat', 'lon'), may hold values from -6 to 6
- params: float32 [307200], P(('lon', 'lat')), may hold values from -1.5 to 1.5
- langevin_noise: float32 [307200], P(('lon', 'lat')), may hold values from -6 to 6
- upstream: bfloat16 [720, 720, 192], P('lat', 'lon'), may hold values from -6 to 6
Outputs:
- output: bfloat16 [720, 720, 192], P('lat', 'lon')
- field_grad: bfloat16 [720, 720, 192], P('lat', 'lon')
- new_params: float32 [307200], P(('lon', 'lat'))
The draws below stay inside these ranges and needn't reach their ends.
All inputs are finite; a program needn't handle non-finite values.
Results may differ from the reference program's by a relative error of at most 0.0085.
Values may be sent and summed in bfloat16 or wider, within the bound.
A program may use at most 64 MiB of HBM per device.

```python
import math
import jax
import jax.numpy as jnp
from jax import lax

C = 192
H = 768
KS = 7
LAT_DEV = 45
LON = 720
LAT = 720
NPAR = 306048
PTOT = 307200


def draw_params(key, part):
    subkeys = jax.random.split(key, 3)
    position = jnp.arange(PTOT, dtype=jnp.int32)
    normal_base = jax.random.truncated_normal(subkeys[0], -3.0, 3.0, (PTOT,), jnp.float32)
    uniform_base = jax.random.uniform(subkeys[1], (PTOT,), jnp.float32, -1.0, 1.0)
    chan_scale = jnp.exp(jax.random.uniform(subkeys[2], (C,), jnp.float32, math.log(0.3), math.log(3.0)))
    end_in = C * H
    end_out = 2 * C * H
    end_kernel = end_out + KS * KS * C
    end_cbias = end_kernel + C
    end_gain = end_cbias + C
    end_shift = end_gain + C
    end_bias_in = end_shift + H
    end_bias_out = end_bias_in + C
    end_scale = end_bias_out + C
    channel = jnp.clip(position - end_out, 0, PTOT) % C
    kernel_vals = normal_base * chan_scale[channel] / KS
    values = jnp.where(position < end_scale, 1.0 + 0.5 * uniform_base, 0.02 * normal_base)
    values = jnp.where(position < end_bias_out, 0.5 * uniform_base, values)
    values = jnp.where(position < end_bias_in, 0.5 * uniform_base, values)
    values = jnp.where(position < end_shift, 0.5 * uniform_base, values)
    values = jnp.where(position < end_gain, 1.0 + 0.5 * uniform_base, values)
    values = jnp.where(position < end_cbias, uniform_base, values)
    values = jnp.where(position < end_kernel, kernel_vals, values)
    values = jnp.where(position < end_out, normal_base * H ** (-0.5), values)
    values = jnp.where(position < end_in, normal_base * C ** (-0.5), values)
    return values.astype(jnp.float32)


def block_levels(key, shape, cuts, low, top_value):
    def one(dim, parts):
        draws = jax.random.uniform(jax.random.fold_in(jax.random.fold_in(key, 6), dim), (parts,), jnp.float32, low / len(cuts), top_value / len(cuts))
        return jnp.repeat(jnp.exp(draws), shape[dim] // parts).reshape((-1,) + (1,) * (len(shape) - dim - 1))

    gain = one(*cuts[0])
    for cut in cuts[1:]:
        gain = gain * one(*cut)
    return gain


def normal_values(rng, dims, scale, limit, shards=(), kind=jnp.bfloat16):
    array = jax.random.normal(rng, dims, jnp.float32) * scale
    if len(shards) > 0:
        array = block_levels(rng, dims, shards, -0.22, 0.18) * array
    return jnp.clip(array, min=-limit, max=limit).astype(kind)


def setup_inputs(seed: int = 0) -> dict:
    key_of = jax.random.split(jax.random.key(seed), 5)
    features = normal_values(key_of[0], (LAT, LON, C), 1.0, 6.0, ((0, 16), (1, 16)))
    params = draw_params(jax.random.fold_in(key_of[4], 71), 0)
    langevin_noise = normal_values(key_of[2], (PTOT,), 1.0, 6.0, ((0, 256),), jnp.float32)
    upstream = normal_values(key_of[3], (LAT, LON, C), 1.0, 6.0, ((0, 16), (1, 16)))
    return dict(features=features, params=params, langevin_noise=langevin_noise, upstream=upstream)


EPSILON = 1e-06
STEP_SIZE = 0.003
NOISE_COEF = 0.08

def unpack(weights):
    layouts = [(C, H), (H, C), (KS, KS, C), (C,), (C,), (C,), (H,), (C,), (C,)]
    pieces = []
    offset = 0
    for layout in layouts:
        length = math.prod(layout)
        pieces.append(weights[offset:offset + length].reshape(layout))
        offset = offset + length
    return pieces

def gelu_tanh(values):
    return jax.nn.gelu(values, approximate=True)

def depthwise(padded, kernel, conv_bias, lat_rows, lon_cols):
    summed = jnp.zeros((lat_rows, lon_cols, padded.shape[2]), jnp.float32) + conv_bias
    for row_off in range(KS):
        for col_off in range(KS):
            window = padded[row_off:row_off + lat_rows, col_off:col_off + lon_cols]
            summed = summed + kernel[row_off, col_off] * window.astype(jnp.float32)
    return summed

def transposed(grad_padded, kernel, lat_rows, lon_cols):
    span = KS - 1
    summed = jnp.zeros((lat_rows, lon_cols, grad_padded.shape[2]), jnp.float32)
    for row_off in range(KS):
        for col_off in range(KS):
            window = grad_padded[span - row_off:span - row_off + lat_rows, span - col_off:span - col_off + lon_cols]
            summed = summed + kernel[row_off, col_off] * window.astype(jnp.float32)
    return summed

def kernel_grad(grad_conv, padded, lat_rows, lon_cols):
    sums = []
    for row_off in range(KS):
        for col_off in range(KS):
            window = padded[row_off:row_off + lat_rows, col_off:col_off + lon_cols]
            sums.append(lax.optimization_barrier(jnp.sum(grad_conv.astype(jnp.float32) * window.astype(jnp.float32), axis=(0, 1))))
    return jnp.stack(sums).reshape(KS, KS, -1)

def ref_layer(convolved, features, upstream, unpacked):
    w_in, w_out, kernel, conv_bias, ln_gain, ln_bias, bias_in, bias_out, layer_scale = unpacked
    lat_rows, lon_cols, channels = convolved.shape
    flat_conv = convolved.reshape(-1, channels)
    mean_val = lax.optimization_barrier(jnp.mean(flat_conv, axis=-1, keepdims=True))
    centred = flat_conv - mean_val
    inv_std = lax.rsqrt(lax.optimization_barrier(jnp.mean(centred * centred, axis=-1, keepdims=True)) + EPSILON)
    standard = centred * inv_std
    normed = (standard * ln_gain + ln_bias).astype(jnp.bfloat16)
    pre_act = jnp.dot(normed, w_in, preferred_element_type=jnp.float32) + bias_in
    activated, pullback = jax.vjp(gelu_tanh, pre_act)
    act_rounded = activated.astype(jnp.bfloat16)
    branch = jnp.dot(act_rounded, w_out, preferred_element_type=jnp.float32) + bias_out
    features_f32 = features.reshape(-1, channels).astype(jnp.float32)
    output = (features_f32 + layer_scale * branch).astype(jnp.bfloat16).reshape(lat_rows, lon_cols, channels)
    upstream_f32 = upstream.reshape(-1, channels).astype(jnp.float32)
    grad_branch = (layer_scale * upstream_f32).astype(jnp.bfloat16)
    grad_act = jnp.dot(grad_branch, w_out.T, preferred_element_type=jnp.float32)
    grad_pre = pullback(grad_act)[0].astype(jnp.bfloat16)
    grad_normed = jnp.dot(grad_pre, w_in.T, preferred_element_type=jnp.float32)
    scaled = grad_normed * ln_gain
    grad_conv = ((scaled - lax.optimization_barrier(jnp.mean(scaled, axis=-1, keepdims=True)) - standard * lax.optimization_barrier(jnp.mean(scaled * standard, axis=-1, keepdims=True))) * inv_std).astype(jnp.bfloat16)
    grad_in_proj = jnp.dot(normed.T, grad_pre, preferred_element_type=jnp.float32)
    grad_out_proj = jnp.dot(act_rounded.T, grad_branch, preferred_element_type=jnp.float32)
    grad_gain = lax.optimization_barrier(jnp.sum(grad_normed * standard, axis=0))
    grad_shift = lax.optimization_barrier(jnp.sum(grad_normed, axis=0))
    grad_bias_in = lax.optimization_barrier(jnp.sum(grad_pre.astype(jnp.float32), axis=0))
    grad_bias_out = lax.optimization_barrier(jnp.sum(grad_branch.astype(jnp.float32), axis=0))
    grad_scale = lax.optimization_barrier(jnp.sum(branch * upstream_f32, axis=0))
    layer_grads = (grad_in_proj, grad_out_proj, grad_gain, grad_shift, grad_bias_in, grad_bias_out, grad_scale)
    return (output, grad_conv.reshape(lat_rows, lon_cols, channels), layer_grads)

def reference(features, params, langevin_noise, upstream):
    weights = params.astype(jnp.bfloat16)
    segments = unpack(weights)
    unpacked = [segments[0], segments[1]] + [segment.astype(jnp.float32) for segment in segments[2:]]
    kernel = unpacked[2]
    conv_bias = unpacked[3]
    half_side = KS // 2

    def pad_field(values):
        wrapped = jnp.concatenate([values[:, LON - half_side:], values, values[:, :half_side]], axis=1)
        return jnp.pad(wrapped, ((half_side, half_side), (0, 0), (0, 0)))
    padded = pad_field(features)
    block_count = LAT // LAT_DEV

    def block_step(running, block_index):
        offset = block_index * LAT_DEV
        rows_pad = lax.dynamic_slice_in_dim(padded, offset, LAT_DEV + KS - 1, 0)
        rows_feat = lax.dynamic_slice_in_dim(features, offset, LAT_DEV, 0)
        rows_up = lax.dynamic_slice_in_dim(upstream, offset, LAT_DEV, 0)
        convolved = depthwise(rows_pad, kernel, conv_bias, LAT_DEV, LON)
        output, grad_conv, layer_grads = ref_layer(convolved, rows_feat, rows_up, unpacked)
        grad_kernel = kernel_grad(grad_conv, rows_pad, LAT_DEV, LON)
        grad_conv_bias = lax.optimization_barrier(jnp.sum(grad_conv.astype(jnp.float32), axis=(0, 1)))
        fresh = layer_grads + (grad_kernel, grad_conv_bias)
        updated = tuple((before_sum + block_sum for before_sum, block_sum in zip(running, fresh)))
        return (updated, (output, grad_conv))
    zeros_init = (jnp.zeros((C, H), jnp.float32), jnp.zeros((H, C), jnp.float32), jnp.zeros((C,), jnp.float32), jnp.zeros((C,), jnp.float32), jnp.zeros((H,), jnp.float32), jnp.zeros((C,), jnp.float32), jnp.zeros((C,), jnp.float32), jnp.zeros((KS, KS, C), jnp.float32), jnp.zeros((C,), jnp.float32))
    running, (out_blocks, grad_blocks) = lax.scan(block_step, zeros_init, jnp.arange(block_count, dtype=jnp.int32))
    output = out_blocks.reshape(LAT, LON, C)
    grad_conv_all = grad_blocks.reshape(LAT, LON, C)
    grad_padded = pad_field(grad_conv_all)

    def input_grad_block(block_index):
        offset = block_index * LAT_DEV
        rows_pad = lax.dynamic_slice_in_dim(grad_padded, offset, LAT_DEV + KS - 1, 0)
        rows_up = lax.dynamic_slice_in_dim(upstream, offset, LAT_DEV, 0)
        return (rows_up.astype(jnp.float32) + transposed(rows_pad, kernel, LAT_DEV, LON)).astype(jnp.bfloat16)
    field_grad = lax.map(input_grad_block, jnp.arange(block_count, dtype=jnp.int32)).reshape(LAT, LON, C)
    grad_in_proj, grad_out_proj, grad_gain, grad_shift, grad_bias_in, grad_bias_out, grad_scale, grad_kernel, grad_conv_bias = running
    flat_grads = jnp.concatenate([grad_in_proj.reshape(-1), grad_out_proj.reshape(-1), grad_kernel.reshape(-1), grad_conv_bias, grad_gain, grad_shift, grad_bias_in, grad_bias_out, grad_scale])
    flat_grads = jnp.pad(flat_grads, (0, PTOT - NPAR))
    new_params = params - STEP_SIZE * flat_grads + NOISE_COEF * langevin_noise
    return (output, field_grad, new_params)
```

```python
import functools

import jax
import jax.numpy as jnp
from jax import lax
from jax.experimental import pallas as pl
from jax.experimental.pallas import tpu as pltpu
from jax.sharding import PartitionSpec as P

C = 192
H = 768
KS = 7

EPSILON = 1e-06
STEP_SIZE = 0.003
NOISE_COEF = 0.08

MESH = pl.DeviceIdType.MESH
SHARD = 1200
NLAT = 16
NLON = 16
GROUP_ROWS = NLAT * SHARD // 128
SLOT = 160
FLAT_ROWS = NLON * GROUP_ROWS
PAD_ROWS = FLAT_ROWS + 16
OUT_ROW = C * H // 128
SMALL_ROW = 2 * C * H // 128
SMALL = 58


def first_row(k):
    return k * SHARD // 128


def greet(axes):
    barrier = pltpu.get_barrier_semaphore()
    count = 0
    for name, size in axes:
        me = lax.axis_index(name)
        for d in range(1, size):
            pl.semaphore_signal(
                barrier, inc=1, device_id={name: lax.rem(me + d, size)}, device_id_type=MESH
            )
            count += 1
    pl.semaphore_wait(barrier, count)


def exchange(name, size, source, target, send_sem, recv_sem):
    me = lax.axis_index(name)
    copies = []
    for d in range(1, size):
        peer = lax.rem(me + d, size)
        copy = pltpu.make_async_remote_copy(
            src_ref=source(peer),
            dst_ref=target(me),
            send_sem=send_sem.at[d],
            recv_sem=recv_sem.at[d],
            device_id={name: peer},
            device_id_type=MESH,
        )
        copy.start()
        copies.append(copy)
    return copies


def lane_offset():
    return lax.rem(lax.axis_index("lat") * (SHARD % 128), 128)


def gather_kernel(
    p_ref, win_ref, wout_ref, small_ref, send1, s1, group, send2, s2, flat, wide,
    ssem1, rsem1, ssem2, rsem2,
):
    lat = lax.axis_index("lat")
    lon = lax.axis_index("lon")
    greet((("lat", NLAT), ("lon", NLON)))
    off = lane_offset()
    rolled = pltpu.roll(p_ref[...], off, 1)
    above = pltpu.roll(rolled, 1, 0)
    lane = lax.broadcasted_iota(jnp.int32, (16, 128), 1)
    block = jnp.where(lane < off, above, rolled).astype(jnp.bfloat16)
    send1[...] = block
    copies = exchange("lat", NLAT, lambda peer: send1, lambda me: s1.at[me], ssem1, rsem1)
    s1[lat] = block
    group[...] = jnp.zeros((SLOT, 128), jnp.float32)
    for copy in copies:
        copy.wait()
    for k in range(NLAT):
        rows = pl.ds(first_row(k), 16)
        group[rows, :] = group[rows, :] + s1[k].astype(jnp.float32)
    packed = group[...].astype(jnp.bfloat16)
    send2[...] = packed
    copies = exchange("lon", NLON, lambda peer: send2, lambda me: s2.at[me], ssem2, rsem2)
    s2[lon] = packed
    for copy in copies:
        copy.wait()
    for k in range(NLON):
        flat[pl.ds(k * GROUP_ROWS, SLOT), :] = s2[k].astype(jnp.float32)
    for j in range(H // 128):
        win_ref[:, pl.ds(128 * j, 128)] = flat[pl.ds(j, C, stride=H // 128), :].astype(jnp.bfloat16)
    unpack_rows(flat, OUT_ROW, H // 2, wide)
    wout_ref[...] = wide[...].astype(jnp.bfloat16)
    unpack_rows(flat, SMALL_ROW, SMALL // 2, small_ref)


def unpack_rows(flat, base, pairs, out):
    first = flat[pl.ds(base, pairs, stride=3), :]
    middle = flat[pl.ds(base + 1, pairs, stride=3), :]
    last = flat[pl.ds(base + 2, pairs, stride=3), :]
    low = lax.broadcasted_iota(jnp.int32, (pairs, 128), 1) < 64
    middle_turned = pltpu.roll(middle, 64, 1)
    last_turned = pltpu.roll(last, 64, 1)
    out[0, 0:pairs, :] = first
    out[0, pairs : 2 * pairs, :] = jnp.where(low, middle_turned, last_turned)
    out[1, 0:pairs, :] = middle
    out[1, pairs : 2 * pairs, :] = last_turned


def pack_rows(flat, base, pairs, values):
    low = lax.broadcasted_iota(jnp.int32, (pairs, 128), 1) < 64
    odd_turned = pltpu.roll(values[0, pairs : 2 * pairs, :], 64, 1)
    odd_tail_turned = pltpu.roll(values[1, pairs : 2 * pairs, :], 64, 1)
    flat[pl.ds(base, pairs, stride=3), :] = values[0, 0:pairs, :]
    flat[pl.ds(base + 1, pairs, stride=3), :] = jnp.where(low, values[1, 0:pairs, :], odd_turned)
    flat[pl.ds(base + 2, pairs, stride=3), :] = jnp.where(low, odd_turned, odd_tail_turned)


def reduce_kernel(
    gin_ref, gout_ref, small_ref, p_ref, noise_ref, new_ref, flat, send1, r1, group, send2, r2,
    ssem1, rsem1, ssem2, rsem2,
):
    lat = lax.axis_index("lat")
    lon = lax.axis_index("lon")
    greet((("lat", NLAT), ("lon", NLON)))
    flat[pl.ds(SMALL_ROW + 80, PAD_ROWS - SMALL_ROW - 80), :] = jnp.zeros(
        (PAD_ROWS - SMALL_ROW - 80, 128), jnp.float32
    )
    for j in range(H // 128):
        flat[pl.ds(j, C, stride=H // 128), :] = gin_ref[:, pl.ds(128 * j, 128)]
    pack_rows(flat, OUT_ROW, H // 2, gout_ref)
    pack_rows(flat, SMALL_ROW, SMALL // 2, small_ref)
    for k in range(NLON):
        send1[k] = flat[pl.ds(k * GROUP_ROWS, SLOT), :].astype(jnp.bfloat16)
    copies = exchange("lon", NLON, lambda peer: send1.at[peer], lambda me: r1.at[me], ssem1, rsem1)
    r1[lon] = send1[lon]
    for copy in copies:
        copy.wait()
    total = r1[0].astype(jnp.float32)
    for k in range(1, NLON):
        total = total + r1[k].astype(jnp.float32)
    group[...] = total
    for k in range(NLAT):
        send2[k] = group[pl.ds(first_row(k), 16), :]
    copies = exchange("lat", NLAT, lambda peer: send2.at[peer], lambda me: r2.at[me], ssem2, rsem2)
    r2[lat] = send2[lat]
    for copy in copies:
        copy.wait()
    total = r2[0]
    for k in range(1, NLAT):
        total = total + r2[k]
    off = lane_offset()
    lane = lax.broadcasted_iota(jnp.int32, (16, 128), 1)
    below = pltpu.roll(total, 15, 0)
    mixed = jnp.where(lane < off, below, total)
    grads = pltpu.roll(mixed, lax.rem(128 - off, 128), 1)
    new_ref[...] = p_ref[...] - STEP_SIZE * grads + NOISE_COEF * noise_ref[...]


VM = pl.BlockSpec(memory_space=pltpu.VMEM)


def comm_params(number):
    return pltpu.CompilerParams(
        collective_id=number, has_side_effects=True, vmem_limit_bytes=48 * 1024 * 1024
    )


def dma(n):
    return pltpu.SemaphoreType.DMA((n,))


def gather_weights(params):
    padded = jnp.pad(params, (0, 2048 - SHARD)).reshape(16, 128)
    return pl.pallas_call(
        gather_kernel,
        out_shape=(
            jax.ShapeDtypeStruct((C, H), jnp.bfloat16),
            jax.ShapeDtypeStruct((2, H, 128), jnp.bfloat16),
            jax.ShapeDtypeStruct((2, SMALL, 128), jnp.float32),
        ),
        in_specs=[VM],
        out_specs=(VM, VM, VM),
        scratch_shapes=[
            pltpu.VMEM((16, 128), jnp.bfloat16),
            pltpu.VMEM((NLAT, 16, 128), jnp.bfloat16),
            pltpu.VMEM((SLOT, 128), jnp.float32),
            pltpu.VMEM((SLOT, 128), jnp.bfloat16),
            pltpu.VMEM((NLON, SLOT, 128), jnp.bfloat16),
            pltpu.VMEM((PAD_ROWS, 128), jnp.float32),
            pltpu.VMEM((2, H, 128), jnp.float32),
            dma(NLAT), dma(NLAT), dma(NLON), dma(NLON),
        ],
        compiler_params=comm_params(0),
        name="gather_weights",
    )(padded)


def reduce_step(grad_in, grad_out, small, params, noise):
    padded = jnp.pad(params, (0, 2048 - SHARD)).reshape(16, 128)
    padded_noise = jnp.pad(noise, (0, 2048 - SHARD)).reshape(16, 128)
    out = pl.pallas_call(
        reduce_kernel,
        out_shape=jax.ShapeDtypeStruct((16, 128), jnp.float32),
        in_specs=[VM] * 5,
        out_specs=VM,
        scratch_shapes=[
            pltpu.VMEM((PAD_ROWS, 128), jnp.float32),
            pltpu.VMEM((NLON, SLOT, 128), jnp.bfloat16),
            pltpu.VMEM((NLON, SLOT, 128), jnp.bfloat16),
            pltpu.VMEM((SLOT, 128), jnp.float32),
            pltpu.VMEM((NLAT, 16, 128), jnp.float32),
            pltpu.VMEM((NLAT, 16, 128), jnp.float32),
            dma(NLON), dma(NLON), dma(NLAT), dma(NLAT),
        ],
        compiler_params=comm_params(1),
        name="reduce_step",
    )(grad_in, grad_out, small, padded, padded_noise)
    return out.reshape(2048)[:SHARD]


def join_rows(halves):
    pairs = halves.shape[1] // 2
    rows = jnp.concatenate([halves[0], halves[1, :, :64]], axis=1)
    return rows.reshape(2, pairs, C).transpose(1, 0, 2).reshape(2 * pairs, C)


def split_rows(rows):
    pairs = rows.shape[0] // 2
    ordered = rows.reshape(pairs, 2, C).transpose(1, 0, 2).reshape(2 * pairs, C)
    return jnp.stack([ordered[:, :128], jnp.pad(ordered[:, 128:], ((0, 0), (0, 64)))])


def padded_2(block, sides, width, periodic):
    for axis, dim in sides:
        count = lax.axis_size(axis)
        forward = [(i, i + 1) for i in range(count - 1)]
        if periodic:
            forward.append((count - 1, 0))
        backward = [(target, source) for source, target in forward]
        low = lax.ppermute(
            lax.slice_in_dim(block, block.shape[dim] - width, None, axis=dim), axis, forward
        )
        high = lax.ppermute(lax.slice_in_dim(block, 0, width, axis=dim), axis, backward)
        block = jnp.concatenate([low, block, high], axis=dim)
    return block


def gelu_tanh(values):
    return jax.nn.gelu(values, approximate=True)


def depthwise(padded, kernel, conv_bias, lat_rows, lon_cols):
    summed = jnp.zeros((lat_rows, lon_cols, padded.shape[2]), jnp.float32) + conv_bias
    for row_off in range(KS):
        for col_off in range(KS):
            window = padded[row_off : row_off + lat_rows, col_off : col_off + lon_cols]
            summed = summed + kernel[row_off, col_off] * window.astype(jnp.float32)
    return summed


def transposed(grad_padded, kernel, lat_rows, lon_cols):
    span = KS - 1
    summed = jnp.zeros((lat_rows, lon_cols, grad_padded.shape[2]), jnp.float32)
    for row_off in range(KS):
        for col_off in range(KS):
            window = grad_padded[
                span - row_off : span - row_off + lat_rows,
                span - col_off : span - col_off + lon_cols,
            ]
            summed = summed + kernel[row_off, col_off] * window.astype(jnp.float32)
    return summed


def kernel_grad(grad_conv, padded, lat_rows, lon_cols):
    sums = []
    for row_off in range(KS):
        for col_off in range(KS):
            window = padded[row_off : row_off + lat_rows, col_off : col_off + lon_cols]
            sums.append(
                jnp.sum(grad_conv.astype(jnp.float32) * window.astype(jnp.float32), axis=(0, 1))
            )
    return jnp.stack(sums)


def layer_pass(convolved, features, upstream, unpacked):
    w_in, w_out, ln_gain, ln_bias, bias_in, bias_out, layer_scale = unpacked
    mean_val = jnp.mean(convolved, axis=-1, keepdims=True)
    centred = convolved - mean_val
    inv_std = lax.rsqrt(jnp.mean(centred * centred, axis=-1, keepdims=True) + EPSILON)
    standard = centred * inv_std
    normed = (standard * ln_gain + ln_bias).astype(jnp.bfloat16)
    pre_act = jnp.einsum("ijc,ch->ijh", normed, w_in, preferred_element_type=jnp.float32) + bias_in
    activated, pullback = jax.vjp(gelu_tanh, pre_act)
    act_rounded = activated.astype(jnp.bfloat16)
    branch = (
        jnp.einsum("ijh,hc->ijc", act_rounded, w_out, preferred_element_type=jnp.float32) + bias_out
    )
    output = (features.astype(jnp.float32) + layer_scale * branch).astype(jnp.bfloat16)
    upstream_f32 = upstream.astype(jnp.float32)
    grad_branch = (layer_scale * upstream_f32).astype(jnp.bfloat16)
    grad_act = jnp.einsum("ijc,hc->ijh", grad_branch, w_out, preferred_element_type=jnp.float32)
    grad_pre = pullback(grad_act)[0].astype(jnp.bfloat16)
    grad_normed = jnp.einsum("ijh,ch->ijc", grad_pre, w_in, preferred_element_type=jnp.float32)
    scaled = grad_normed * ln_gain
    grad_conv = (
        (
            scaled
            - jnp.mean(scaled, axis=-1, keepdims=True)
            - standard * jnp.mean(scaled * standard, axis=-1, keepdims=True)
        )
        * inv_std
    ).astype(jnp.bfloat16)
    grad_in_proj = jnp.einsum("ijc,ijh->ch", normed, grad_pre, preferred_element_type=jnp.float32)
    grad_out_proj = jnp.einsum(
        "ijh,ijc->hc", act_rounded, grad_branch, preferred_element_type=jnp.float32
    )
    grad_gain = jnp.sum(grad_normed * standard, axis=(0, 1))
    grad_shift = jnp.sum(grad_normed, axis=(0, 1))
    grad_bias_in = jnp.sum(grad_pre.astype(jnp.float32), axis=(0, 1))
    grad_bias_out = jnp.sum(grad_branch.astype(jnp.float32), axis=(0, 1))
    grad_scale = jnp.sum(branch * upstream_f32, axis=(0, 1))
    layer_grads = (
        grad_in_proj,
        grad_out_proj,
        grad_gain,
        grad_shift,
        grad_bias_in,
        grad_bias_out,
        grad_scale,
    )
    return (output, grad_conv, layer_grads)


def body(features, params, langevin_noise, upstream):
    lat_rows = features.shape[0]
    lon_cols = features.shape[1]
    half_side = KS // 2
    w_in, w_out_halves, small_halves = gather_weights(params)
    w_out = join_rows(w_out_halves)
    small = join_rows(small_halves)
    kernel = small[: KS * KS].reshape(KS, KS, C)
    conv_bias, ln_gain, ln_bias = small[49], small[50], small[51]
    bias_in = small[52:56].reshape(H)
    bias_out, layer_scale = small[56], small[57]
    lon_padded = padded_2(features, (("lon", 1),), half_side, True)
    padded = padded_2(lon_padded, (("lat", 0),), half_side, False)
    convolved = depthwise(padded, kernel, conv_bias, lat_rows, lon_cols)
    output, grad_conv, layer_grads = layer_pass(
        convolved, features, upstream, (w_in, w_out, ln_gain, ln_bias, bias_in, bias_out, layer_scale)
    )
    grad_kernel = kernel_grad(grad_conv, padded, lat_rows, lon_cols)
    grad_conv_bias = jnp.sum(grad_conv.astype(jnp.float32), axis=(0, 1))
    grad_lon = padded_2(grad_conv, (("lon", 1),), half_side, True)
    grad_padded = padded_2(grad_lon, (("lat", 0),), half_side, False)
    field_grad = (
        upstream.astype(jnp.float32) + transposed(grad_padded, kernel, lat_rows, lon_cols)
    ).astype(jnp.bfloat16)
    grad_in_proj, grad_out_proj, grad_gain, grad_shift, grad_bias_in, grad_bias_out, grad_scale = (
        layer_grads
    )
    small_grads = jnp.concatenate(
        [
            grad_kernel,
            grad_conv_bias[None],
            grad_gain[None],
            grad_shift[None],
            grad_bias_in.reshape(4, C),
            grad_bias_out[None],
            grad_scale[None],
        ]
    )
    new_params = reduce_step(
        grad_in_proj, split_rows(grad_out_proj), split_rows(small_grads), params, langevin_noise
    )
    return (output, field_grad, new_params)


def solution(mesh):
    return jax.shard_map(
        body,
        mesh=mesh,
        in_specs=(
            P("lat", "lon", None),
            P(("lon", "lat")),
            P(("lon", "lat")),
            P("lat", "lon", None),
        ),
        out_specs=(P("lat", "lon", None), P("lat", "lon", None), P(("lon", "lat"))),
        check_vma=False,
    )
```

```python
import functools
import math

import jax
import jax.numpy as jnp
from jax import lax
from jax.experimental import pallas as pl
from jax.experimental.pallas import tpu as pltpu
from jax.sharding import PartitionSpec as P

C = 192
H = 768
KS = 7
EPSILON = 1e-06
STEP_SIZE = 0.003
NOISE_COEF = 0.08
ROOT = math.sqrt(2.0 / math.pi)
CUBIC = 0.044715

MESH = pl.DeviceIdType.MESH
F32 = jnp.float32
BF16 = jnp.bfloat16
SHARD = 1200
NLAT = 16
NLON = 16
GROUP_ROWS = NLAT * SHARD // 128
HALF_ROWS = GROUP_ROWS // 2
SLOT = 80
FLAT_ROWS = 2416
OUT_ROW = C * H // 128
SMALL_ROW = 2 * C * H // 128
BIAS_IN_ROW = SMALL_ROW + 52 * C // 128
SMALL = 58
HALF_SMALL = SMALL // 2

SIDE = 45
PITCH = SIDE + KS - 1
STRIP = 6
XROWS = 2760
CELLS = SIDE * SIDE
FLAT_CELLS = 8 * STRIP * SIDE
BLOCK = 512
HALF_COLS = 22

EDGES = ((-1, 0), (1, 0), (0, -1), (0, 1))
CORNERS = ((-1, -1), (-1, 1), (1, -1), (1, 1))


def first_row(k):
    return k * SHARD // 128


def small_row(r):
    return (r % 2) * HALF_SMALL + r // 2


def low_lanes(rows):
    return lax.broadcasted_iota(jnp.int32, (rows, 128), 1) < 64


def wrapped(name, size, step):
    return lax.rem(lax.axis_index(name) + step + size, size)


def remote(source, target, send_sem, recv_sem, device):
    return pltpu.make_async_remote_copy(
        src_ref=source,
        dst_ref=target,
        send_sem=send_sem,
        recv_sem=recv_sem,
        device_id=device,
        device_id_type=MESH,
    )


def signal_all():
    barrier = pltpu.get_barrier_semaphore()
    devices = [{"lat": wrapped("lat", NLAT, d)} for d in range(1, NLAT)]
    devices += [{"lon": wrapped("lon", NLON, d)} for d in range(1, NLON)]
    devices += [
        {"lat": wrapped("lat", NLAT, a), "lon": wrapped("lon", NLON, b)} for a, b in CORNERS
    ]
    for device in devices:
        pl.semaphore_signal(barrier, inc=1, device_id=device, device_id_type=MESH)
    return barrier, len(devices)


def halo_copies(edge, corner, edge_in, corner_in, send_sem, recv_sem):
    copies = []
    for q, (a, b) in enumerate(EDGES + CORNERS):
        device = {"lat": wrapped("lat", NLAT, a), "lon": wrapped("lon", NLON, b)}
        source, target = (edge, edge_in) if q < 4 else (corner, corner_in)
        slot = q % 4
        copies.append(
            remote(source.at[slot], target.at[slot], send_sem.at[q], recv_sem.at[q], device)
        )
    return copies


def pack_halo(x, edge, corner):
    for t in range(2):
        lanes = pl.ds(128 * t, 128)
        for n in range(3):
            for q, start in enumerate((3, 45)):
                edge[q, n, :, lanes] = x[t, pl.ds((start + n) * PITCH + 3, 48), :].astype(BF16)
            for q, start in enumerate((3, 45)):
                edge[2 + q, n, :, lanes] = x[
                    t, pl.ds(3 * PITCH + start + n, 48, stride=PITCH), :
                ].astype(BF16)
            for q, (a, b) in enumerate(CORNERS):
                row = 3 if a < 0 else 45
                col = 3 if b < 0 else 45
                corner[q, n, :, lanes] = x[t, pl.ds((row + n) * PITCH + col, 16), :].astype(BF16)


def unpack_halo(x, edge_in, corner_in):
    lat = lax.axis_index("lat")
    keep_top = jnp.where(lat > 0, 1.0, 0.0).astype(F32)
    keep_bottom = jnp.where(lat < NLAT - 1, 1.0, 0.0).astype(F32)
    for t in range(2):
        lanes = pl.ds(128 * t, 128)
        for n in range(3):
            for q, (row, keep) in enumerate(((48, keep_bottom), (0, keep_top))):
                x[t, pl.ds((row + n) * PITCH + 3, SIDE), :] = (
                    edge_in[q, n, :, lanes].astype(F32)[:SIDE] * keep
                )
            for q, col in enumerate((48, 0)):
                x[t, pl.ds(3 * PITCH + col + n, SIDE, stride=PITCH), :] = edge_in[
                    2 + q, n, :, lanes
                ].astype(F32)[:SIDE]
            for q, (a, b) in enumerate(CORNERS):
                row, keep = (48, keep_bottom) if a < 0 else (0, keep_top)
                col = 48 if b < 0 else 0
                x[t, pl.ds((row + n) * PITCH + col, 3), :] = (
                    corner_in[q, n, :, lanes].astype(F32)[:3] * keep
                )


def clear(ref, rows):
    for t in range(2):
        ref[t] = jnp.zeros((rows, 128), F32)


def pair_columns(ref, rows):
    def step(n, _):
        here = pl.ds(pl.multiple_of(n * 40, 8), 40)
        ahead = ref[1, pl.ds(n * 40 + HALF_COLS, 40), :]
        ref[1, here, :] = jnp.where(low_lanes(40), ref[1, here, :], pltpu.roll(ahead, 64, 1))
        return 0

    lax.fori_loop(0, rows // 40, step, 0)


def conv_tile(x, w, t, flip, bias_row, emit):
    def step(jj, _):
        j = jj * 3
        if t == 1:
            j = jnp.minimum(j, HALF_COLS - 2)
        if bias_row is None:
            start = jnp.zeros((8, 128), F32)
        else:
            start = w[t, pl.ds(bias_row, 8, stride=0), :]
        accs = [[start] * STRIP for _ in range(3)]
        for b in range(KS):
            ws = []
            for a in range(KS):
                r = (KS - 1 - a) * KS + KS - 1 - b if flip else a * KS + b
                ws.append(w[t, pl.ds(small_row(r), 8, stride=0), :])
            for c in range(3):
                for rr in range(STRIP + KS - 1):
                    v = x[t, pl.ds(rr * PITCH + j + b + c, 8, stride=STRIP * PITCH), :]
                    for a in range(KS):
                        if 0 <= rr - a < STRIP:
                            accs[c][rr - a] = accs[c][rr - a] + ws[a] * v
        for c in range(3):
            for r in range(STRIP):
                emit(r, j + c, accs[c][r])
        return 0

    lax.fori_loop(0, 15 if t == 0 else 8, step, 0)


def column_slice(r, j):
    return pl.ds(r * SIDE + j, 8, stride=STRIP * SIDE)


def emit_into(out, t):
    def emit(r, j, value):
        if t == 0:
            out[0, column_slice(r, j), :] = value
        else:
            low = low_lanes(8)
            out[1, column_slice(r, j), :] = jnp.where(low, value, 0.0)
            out[1, column_slice(r, j + HALF_COLS), :] = jnp.where(
                low, pltpu.roll(value, 64, 1), 0.0
            )

    return emit


def kernel_grad_tile(x, g, t, gk):
    count = SIDE if t == 0 else HALF_COLS + 1

    def per_col(b, _):
        def step(j, accs):
            accs = list(accs)
            gs = [g[t, column_slice(r, j), :] for r in range(STRIP)]
            for rr in range(STRIP + KS - 1):
                v = x[t, pl.ds(rr * PITCH + j + b, 8, stride=STRIP * PITCH), :]
                for a in range(KS):
                    if 0 <= rr - a < STRIP:
                        accs[a] = accs[a] + gs[rr - a] * v
            return tuple(accs)

        accs = tuple(jnp.zeros((8, 128), F32) for _ in range(KS))
        start = 0
        if t == 1:
            accs = step(0, accs)
            accs = step(1, accs)
            start = 2
        accs = lax.fori_loop(0, (count - start) // 3, lambda n, s: step3(n, s, step, start), accs)
        for a in range(KS):
            total = jnp.sum(accs[a], axis=0, keepdims=True)
            if t == 1:
                total = total + pltpu.roll(total, 64, 1)
            gk[t, pl.ds(b * 8 + a, 1), :] = total
        return 0

    lax.fori_loop(0, KS, per_col, 0)


def step3(n, accs, step, start):
    for c in range(3):
        accs = step(3 * n + c + start, accs)
    return accs


def step_kernel(
    feat_hbm, up_hbm, p_ref, noise_ref, out_hbm, fgrad_hbm, new_ref,
    feat, ups, outb, fgb, x, gp, o, gf, uf,
    win, wout, wide, ws, wz, flat,
    nrm, std, inv, pre, gact, act, gpre, gb, gwin, gwt, sg, gk, sums,
    pad_p, pad_n, send1, s1, s2, group,
    sh, xr, sb, r1, send3, r3,
    edge, corner, edge_in, corner_in, edge2, corner2, edge2_in, corner2_in,
    io_sem, ss1, rs1, ss2, rs2, fs, fr, hs, hr, hs2, hr2, xs, xrs, ls, lr, ss3, rs3,
):
    lat = lax.axis_index("lat")
    lon = lax.axis_index("lon")
    core = lax.rem(lat, 2)
    chip = lax.div(lat, 2)
    half = lax.div(lat, 8)
    place = lax.rem(lat, 8)
    partner = {"lat": lat + 1 - 2 * core}

    feat_copy = pltpu.make_async_copy(feat_hbm, feat, io_sem.at[0])
    up_copy = pltpu.make_async_copy(up_hbm, ups, io_sem.at[1])
    feat_copy.start()
    up_copy.start()
    barrier, count = signal_all()

    for ref, padded in ((p_ref, pad_p), (noise_ref, pad_n)):
        padded[...] = jnp.zeros((16, 128), F32)
        for r in range(9):
            padded[r, :] = ref[pl.ds(128 * r, 128)]
        padded[9, 0:48] = ref[pl.ds(1152, 48)]
    off = lax.rem(lat * (SHARD % 128), 128)
    lane = lax.broadcasted_iota(jnp.int32, (16, 128), 1)
    rolled = pltpu.roll(pad_p[...], off, 1)
    block = jnp.where(lane < off, pltpu.roll(rolled, 1, 0), rolled).astype(BF16)
    send1[...] = block
    pl.semaphore_wait(barrier, count)

    shard_copies = []
    for q in range(8):
        peer = 2 * q + half
        copy = remote(send1, s1.at[place], ss1.at[q], rs1.at[place], {"lat": peer})
        shard_copies.append((peer, copy))
        pl.when(peer != lat)(copy.start)

    @pl.when(half == core)
    def _():
        s1[place] = block

    clear(x, XROWS)
    feat_copy.wait()

    def load_row(i, _):
        row = feat[i].astype(F32)
        x[0, pl.ds((i + 3) * PITCH + 3, SIDE), :] = row[:, :128]
        x[1, pl.ds((i + 3) * PITCH + 3, SIDE), 0:64] = row[:, 128:]
        return 0

    lax.fori_loop(0, SIDE, load_row, 0)
    pack_halo(x, edge, corner)
    halo = halo_copies(edge, corner, edge_in, corner_in, hs, hr)
    for copy in halo:
        copy.start()

    group[...] = jnp.zeros((88, 128), F32)
    for m in range(8):
        source = 8 * core + m
        pl.when(source != lat)(
            remote(send1, s1.at[m], ss1.at[m], rs1.at[m], {"lat": lat}).wait_recv
        )
    for m in range(8):
        rows = pl.ds(first_row(m), 16)
        group[rows, :] = group[rows, :] + s1[m].astype(F32)
    s2[core, lon] = group[0:SLOT, :].astype(BF16)
    for peer, copy in shard_copies:
        pl.when(peer != lat)(copy.wait_send)
    spread = []
    for d in range(1, NLON):
        copy = remote(
            s2.at[core, lon], s2.at[core, lon], ss2.at[d], rs2.at[lon], {"lon": wrapped("lon", NLON, d)}
        )
        copy.start()
        spread.append(copy)

    clear(uf, FLAT_CELLS)
    up_copy.wait()

    def load_up(i, _):
        row = ups[i].astype(F32)
        uf[0, pl.ds(i * SIDE, SIDE), :] = row[:, :128]
        uf[1, pl.ds(i * SIDE, SIDE), 0:64] = row[:, 128:]
        return 0

    lax.fori_loop(0, SIDE, load_up, 0)
    clear(gp, XROWS)
    gwin[...] = jnp.zeros((256, H), F32)
    gwt[...] = jnp.zeros((256, H), F32)
    sums[...] = jnp.zeros((2, 64, 128), F32)
    for copy in halo:
        copy.wait()
    unpack_halo(x, edge_in, corner_in)
    pair_columns(x, 2720)

    def forward(s):
        pl.when(lon != s)(
            remote(s2.at[core, s], s2.at[core, s], ss2.at[0], rs2.at[s], {"lon": lon}).wait_recv
        )
        copy = remote(s2.at[core, s], s2.at[core, s], fs.at[s], fr.at[s], partner)
        copy.start()
        return copy

    def place_group(s):
        for h in range(2):
            flat[pl.ds(s * GROUP_ROWS + h * HALF_ROWS, SLOT), :] = s2[h, s].astype(F32)

    last = forward(NLON - 1)
    last.wait_send()
    remote(s2.at[1 - core, NLON - 1], s2.at[1 - core, NLON - 1], fs.at[NLON - 1], fr.at[NLON - 1], partner).wait_recv()
    place_group(NLON - 1)
    for t, small in enumerate(unpack_pairs(flat, SMALL_ROW, HALF_SMALL)):
        for parity in range(2):
            value = small[parity]
            if t == 1:
                low = low_lanes(HALF_SMALL)
                wz[1, parity * HALF_SMALL : (parity + 1) * HALF_SMALL, :] = jnp.where(low, value, 0.0)
                value = jnp.where(low, value, pltpu.roll(value, 64, 1))
            else:
                wz[0, parity * HALF_SMALL : (parity + 1) * HALF_SMALL, :] = value
            ws[t, parity * HALF_SMALL : (parity + 1) * HALF_SMALL, :] = value

    bias_row = small_row(49)
    conv_tile(x, ws, 0, False, bias_row, emit_into(o, 0))
    passed = [forward(s) for s in range(NLON - 1)]
    conv_tile(x, ws, 1, False, bias_row, emit_into(o, 1))
    for s, copy in enumerate(passed):
        copy.wait_send()
        remote(s2.at[1 - core, s], s2.at[1 - core, s], fs.at[s], fr.at[s], partner).wait_recv()
    for copy in spread:
        copy.wait_send()
    for s in range(NLON):
        place_group(s)

    win[192:256, :] = jnp.zeros((64, H), BF16)
    first = lax.broadcasted_iota(jnp.int32, (16, 128), 0) == 0
    for j in range(H // 128):
        lanes = pl.ds(128 * j, 128)
        win[0:C, lanes] = flat[pl.ds(j, C, stride=H // 128), :].astype(BF16)
        bias = flat[pl.ds(BIAS_IN_ROW + j, 16, stride=0), :]
        win[192:208, lanes] = jnp.where(first, bias, 0.0).astype(BF16)
    for t, values in enumerate(unpack_pairs(flat, OUT_ROW, H // 2)):
        for parity in range(2):
            wide[t, pl.ds(parity, H // 2, stride=2), :] = values[parity]
    wout[:, 0:128] = wide[0].astype(BF16)
    wout[:, 128:256] = jnp.where(low_lanes(H), wide[1], 0.0).astype(BF16)

    gain = [wz[t, small_row(50) : small_row(50) + 1, :] for t in range(2)]
    shift = [wz[t, small_row(51) : small_row(51) + 1, :] for t in range(2)]
    bias_out = [wz[t, small_row(56) : small_row(56) + 1, :] for t in range(2)]
    scale = [wz[t, small_row(57) : small_row(57) + 1, :] for t in range(2)]

    def mean(values):
        return jnp.sum(values[0] + values[1], axis=1, keepdims=True) * (1.0 / C)

    def fold(value):
        return jnp.sum(value.reshape(-1, 8, 128), axis=0)

    def mlp_block(n, _):
        base = n * BLOCK

        def norm_strip(s, _):
            rows = pl.ds(pl.multiple_of(base + s * 64, 64), 64)
            local = pl.ds(pl.multiple_of(s * 64, 64), 64)
            low = low_lanes(64)
            conv = [o[t, rows, :] for t in range(2)]
            m = mean(conv)
            centred = [conv[0] - m, jnp.where(low, conv[1] - m, 0.0)]
            inverse = lax.rsqrt(mean([v * v for v in centred]) + EPSILON)
            inv[local, :] = jnp.broadcast_to(inverse, (64, 128))
            for t in range(2):
                standard = centred[t] * inverse
                std[t, local, :] = standard
                value = standard * gain[t] + shift[t]
                if t == 1:
                    ones = lax.broadcasted_iota(jnp.int32, (64, 128), 1) == 64
                    value = jnp.where(ones, 1.0, value)
                nrm[local, 128 * t : 128 * t + 128] = value.astype(BF16)
                gb[local, 128 * t : 128 * t + 128] = (scale[t] * uf[t, rows, :]).astype(BF16)
            return 0

        lax.fori_loop(0, BLOCK // 64, norm_strip, 0)
        pre[...] = jnp.dot(nrm[...], win[...], preferred_element_type=F32)
        gact[...] = lax.dot_general(
            gb[...], wout[...], (((1,), (1,)), ((), ())), preferred_element_type=F32
        )

        def gelu_strip(s, _):
            local = pl.ds(pl.multiple_of(s * 16, 16), 16)
            for j in range(2):
                lanes = pl.ds(384 * j, 384)
                v = pre[local, lanes]
                square = v * v
                t = jnp.tanh(v * (ROOT + (ROOT * CUBIC) * square))
                hv = 0.5 * v
                act[local, lanes] = (hv + hv * t).astype(BF16)
                slope = 0.5 + 0.5 * t + hv * (1.0 - t * t) * (ROOT + (3.0 * ROOT * CUBIC) * square)
                gpre[local, lanes] = (gact[local, lanes] * slope).astype(BF16)
            return 0

        lax.fori_loop(0, BLOCK // 16, gelu_strip, 0)
        pre[:, 0:256] = jnp.dot(act[...], wout[...], preferred_element_type=F32)
        pre[:, 256:512] = lax.dot_general(
            gpre[...], win[...], (((1,), (1,)), ((), ())), preferred_element_type=F32
        )
        gwin[...] += lax.dot_general(
            nrm[...], gpre[...], (((0,), (0,)), ((), ())), preferred_element_type=F32
        )
        gwt[...] += lax.dot_general(
            gb[...], act[...], (((0,), (0,)), ((), ())), preferred_element_type=F32
        )

        def back_strip(s, totals):
            rows = pl.ds(pl.multiple_of(base + s * 64, 64), 64)
            local = pl.ds(pl.multiple_of(s * 64, 64), 64)
            totals = list(totals)
            low = low_lanes(64)
            scaled, standard = [], []
            for t in range(2):
                branch = pre[local, 128 * t : 128 * t + 128] + bias_out[t]
                o[t, rows, :] = scale[t] * branch
                st = std[t, local, :]
                gn = pre[local, 256 + 128 * t : 384 + 128 * t]
                totals[4 * t] += fold(gn * st)
                totals[4 * t + 1] += fold(gn)
                totals[4 * t + 2] += fold(gb[local, 128 * t : 128 * t + 128].astype(F32))
                totals[4 * t + 3] += fold(branch * uf[t, rows, :])
                scaled.append(gn * gain[t])
                standard.append(st)
            m1 = mean(scaled)
            m2 = mean([a * b for a, b in zip(scaled, standard)])
            inverse = inv[local, :]
            for t in range(2):
                g = ((scaled[t] - m1 - standard[t] * m2) * inverse).astype(BF16).astype(F32)
                gf[t, rows, :] = g if t == 0 else jnp.where(low, g, 0.0)
            return tuple(totals)

        zeros = tuple(jnp.zeros((8, 128), F32) for _ in range(8))
        totals = lax.fori_loop(0, BLOCK // 64, back_strip, zeros)
        for k in range(8):
            rows = pl.ds(8 * (k % 4), 8)
            sums[k // 4, rows, :] = sums[k // 4, rows, :] + totals[k]
        return 0

    lax.fori_loop(0, 4, mlp_block, 0)
    for t in range(2):
        gf[t, 2048:FLAT_CELLS, :] = jnp.zeros((FLAT_CELLS - 2048, 128), F32)

    def grad_row(i, _):
        for t in range(2):
            gp[t, pl.ds((i + 3) * PITCH + 3, SIDE), :] = gf[t, pl.ds(i * SIDE, SIDE), :]
        return 0

    lax.fori_loop(0, SIDE, grad_row, 0)
    pack_halo(gp, edge2, corner2)
    halo2 = halo_copies(edge2, corner2, edge2_in, corner2_in, hs2, hr2)
    for copy in halo2:
        copy.start()

    for j in range(H // 128):
        flat[pl.ds(j, C, stride=H // 128), :] = gwin[0:C, 128 * j : 128 * j + 128]
    wide[0] = jnp.transpose(gwt[0:128, :])
    wide[1] = jnp.transpose(gwt[128:256, :])
    pack_pairs(
        flat, OUT_ROW, H // 2,
        [[wide[t, pl.ds(parity, H // 2, stride=2), :] for parity in range(2)] for t in range(2)],
    )

    def stage_half(l):
        for h in range(2):
            sh[h, l] = flat[pl.ds(l * GROUP_ROWS + h * HALF_ROWS, SLOT), :].astype(BF16)

    for l in range(NLON - 1):
        stage_half(l)
    bulk = remote(
        sh.at[1 - core, pl.ds(0, NLON - 1)], xr.at[pl.ds(0, NLON - 1)], xs.at[0], xrs.at[0], partner
    )
    bulk.start()

    def out_row(i, _):
        row = feat[i].astype(F32)
        rows = pl.ds(i * SIDE, SIDE)
        outb[i, :, 0:128] = (row[:, :128] + o[0, rows, :]).astype(BF16)
        outb[i, :, 128:192] = (row[:, 128:] + o[1, rows, :][:, :64]).astype(BF16)
        return 0

    lax.fori_loop(0, SIDE, out_row, 0)
    out_copy = pltpu.make_async_copy(outb, out_hbm, io_sem.at[2])
    out_copy.start()

    for t in range(2):
        total = jnp.sum(gf[t].reshape(-1, 8, 128), axis=0)
        sums[t, 32:40, :] = total
    pair_columns(gf, 2120)
    column = gf[1, pl.ds(0, SIDE, stride=SIDE), :]
    gf[1, pl.ds(0, SIDE, stride=SIDE), :] = jnp.where(low_lanes(SIDE), column, 0.0)

    kernel_grad_tile(x, gf, 0, gk)
    bulk.wait()

    def add_half(l):
        return (sh[core, l].astype(F32) + xr[l].astype(F32)).astype(BF16)

    for l in range(NLON - 1):
        sb[l] = add_half(l)
    blocks = []
    for l in range(NLON):
        blocks.append(remote(sb.at[l], r1.at[lon], ls.at[l], lr.at[lon], {"lon": l}))
    for l in range(NLON - 1):
        pl.when(lon != l)(blocks[l].start)

        @pl.when(lon == l)
        def _():
            r1[l] = sb[l]

    kernel_grad_tile(x, gf, 1, gk)

    for t in range(2):
        for r in range(KS * KS):
            sg[t, small_row(r), :] = gk[t, (r % KS) * 8 + r // KS, :]
        for r, k in ((49, 4), (50, 0), (51, 1), (56, 2), (57, 3)):
            sg[t, small_row(r), :] = jnp.sum(sums[t, 8 * k : 8 * k + 8, :], axis=0)
        for r in range(52, 56):
            sg[t, small_row(r), :] = jnp.zeros((128,), F32)
    flat[pl.ds(SMALL_ROW + 80, FLAT_ROWS - SMALL_ROW - 80), :] = jnp.zeros(
        (FLAT_ROWS - SMALL_ROW - 80, 128), F32
    )
    pack_pairs(
        flat, SMALL_ROW, HALF_SMALL,
        [
            [sg[t, parity * HALF_SMALL : (parity + 1) * HALF_SMALL, :] for parity in range(2)]
            for t in range(2)
        ],
    )
    for j in range(H // 128):
        flat[BIAS_IN_ROW + j, :] = gwin[192, 128 * j : 128 * j + 128]
    stage_half(NLON - 1)
    tail = remote(sh.at[1 - core, NLON - 1], xr.at[NLON - 1], xs.at[1], xrs.at[1], partner)
    tail.start()

    for copy in halo2:
        copy.wait()
    unpack_halo(gp, edge2_in, corner2_in)
    pair_columns(gp, 2720)
    tail.wait()
    sb[NLON - 1] = add_half(NLON - 1)
    pl.when(lon != NLON - 1)(blocks[NLON - 1].start)

    @pl.when(lon == NLON - 1)
    def _():
        r1[NLON - 1] = sb[NLON - 1]

    conv_tile(gp, ws, 0, True, None, emit_into(o, 0))
    conv_tile(gp, ws, 1, True, None, emit_into(o, 1))

    def grad_out_row(i, _):
        row = ups[i].astype(F32)
        rows = pl.ds(i * SIDE, SIDE)
        fgb[i, :, 0:128] = (row[:, :128] + o[0, rows, :]).astype(BF16)
        fgb[i, :, 128:192] = (row[:, 128:] + o[1, rows, :][:, :64]).astype(BF16)
        return 0

    lax.fori_loop(0, SIDE, grad_out_row, 0)
    fgrad_copy = pltpu.make_async_copy(fgb, fgrad_hbm, io_sem.at[3])
    fgrad_copy.start()

    for s in range(NLON):
        pl.when(lon != s)(remote(sb.at[s], r1.at[s], ls.at[s], lr.at[s], {"lon": lon}).wait_recv)
    total = r1[0].astype(F32)
    for s in range(1, NLON):
        total = total + r1[s].astype(F32)
    group[0:SLOT, :] = total
    for m in range(8):
        send3[m] = group[pl.ds(first_row(m), 16), :]
    pieces = []
    for m in range(8):
        owner = 8 * core + m
        copy = remote(send3.at[m], r3.at[chip], ss3.at[m], rs3.at[chip], {"lat": owner})
        pieces.append((owner, copy))
        pl.when(owner != lat)(copy.start)

    @pl.when(half == core)
    def _():
        r3[chip] = send3[place]

    for q in range(8):
        source = 2 * q + half
        pl.when(source != lat)(
            remote(send3.at[q], r3.at[q], ss3.at[q], rs3.at[q], {"lat": lat}).wait_recv
        )
    total = r3[0]
    for q in range(1, 8):
        total = total + r3[q]
    mixed = jnp.where(lane < off, pltpu.roll(total, 15, 0), total)
    grads = pltpu.roll(mixed, lax.rem(128 - off, 128), 1)
    pad_p[...] = pad_p[...] - STEP_SIZE * grads + NOISE_COEF * pad_n[...]
    for r in range(9):
        new_ref[pl.ds(128 * r, 128)] = pad_p[r, :]
    new_ref[pl.ds(1152, 48)] = pad_p[9, 0:48]
    for l in range(NLON):
        pl.when(lon != l)(blocks[l].wait_send)
    for owner, copy in pieces:
        pl.when(owner != lat)(copy.wait_send)
    out_copy.wait()
    fgrad_copy.wait()


def unpack_pairs(flat, base, pairs):
    first = flat[pl.ds(base, pairs, stride=3), :]
    middle = flat[pl.ds(base + 1, pairs, stride=3), :]
    last = flat[pl.ds(base + 2, pairs, stride=3), :]
    last_turned = pltpu.roll(last, 64, 1)
    odd = jnp.where(low_lanes(pairs), pltpu.roll(middle, 64, 1), last_turned)
    return [[first, odd], [middle, last_turned]]


def pack_pairs(flat, base, pairs, values):
    low = low_lanes(pairs)
    odd_turned = pltpu.roll(values[0][1], 64, 1)
    tail_turned = pltpu.roll(values[1][1], 64, 1)
    flat[pl.ds(base, pairs, stride=3), :] = values[0][0]
    flat[pl.ds(base + 1, pairs, stride=3), :] = jnp.where(low, values[1][0], odd_turned)
    flat[pl.ds(base + 2, pairs, stride=3), :] = jnp.where(low, odd_turned, tail_turned)


VM = pl.BlockSpec(memory_space=pltpu.VMEM)
ANY = pl.BlockSpec(memory_space=pl.ANY)


def vm(*shape, kind=F32):
    return pltpu.VMEM(shape, kind)


def dma(n):
    return pltpu.SemaphoreType.DMA((n,))


def body(features, params, langevin_noise, upstream):
    field = features.shape
    halo_shapes = [
        vm(4, 3, 48, 256, kind=BF16), vm(4, 3, 16, 256, kind=BF16),
        vm(4, 3, 48, 256, kind=BF16), vm(4, 3, 16, 256, kind=BF16),
    ]
    return pl.pallas_call(
        step_kernel,
        out_shape=(
            jax.ShapeDtypeStruct(field, BF16),
            jax.ShapeDtypeStruct(field, BF16),
            jax.ShapeDtypeStruct(params.shape, F32),
        ),
        in_specs=[ANY, ANY, VM, VM],
        out_specs=(ANY, ANY, VM),
        scratch_shapes=[
            vm(*field, kind=BF16), vm(*field, kind=BF16), vm(*field, kind=BF16), vm(*field, kind=BF16),
            vm(2, XROWS, 128), vm(2, XROWS, 128),
            vm(2, FLAT_CELLS, 128), vm(2, FLAT_CELLS, 128), vm(2, FLAT_CELLS, 128),
            vm(256, H, kind=BF16), vm(H, 256, kind=BF16), vm(2, H, 128),
            vm(2, 64, 128), vm(2, 64, 128), vm(FLAT_ROWS, 128),
            vm(BLOCK, 256, kind=BF16), vm(2, BLOCK, 128), vm(BLOCK, 128),
            vm(BLOCK, H), vm(BLOCK, H), vm(BLOCK, H, kind=BF16), vm(BLOCK, H, kind=BF16),
            vm(BLOCK, 256, kind=BF16), vm(256, H), vm(256, H), vm(2, 64, 128), vm(2, 64, 128),
            vm(2, 64, 128),
            vm(16, 128), vm(16, 128), vm(16, 128, kind=BF16), vm(8, 16, 128, kind=BF16),
            vm(2, NLON, SLOT, 128, kind=BF16), vm(88, 128),
            vm(2, NLON, SLOT, 128, kind=BF16), vm(NLON, SLOT, 128, kind=BF16),
            vm(NLON, SLOT, 128, kind=BF16), vm(NLON, SLOT, 128, kind=BF16),
            vm(8, 16, 128), vm(8, 16, 128),
            *halo_shapes, *halo_shapes,
            dma(4), dma(8), dma(8), dma(NLON), dma(NLON), dma(NLON), dma(NLON),
            dma(8), dma(8), dma(8), dma(8), dma(2), dma(2), dma(NLON), dma(NLON), dma(8), dma(8),
        ],
        compiler_params=pltpu.CompilerParams(
            collective_id=0, has_side_effects=True, vmem_limit_bytes=60 * 1024 * 1024
        ),
        name="langevin_step",
    )(features, upstream, params, langevin_noise)


def solution(mesh):
    return jax.shard_map(
        body,
        mesh=mesh,
        in_specs=(
            P("lat", "lon", None),
            P(("lon", "lat")),
            P(("lon", "lat")),
            P("lat", "lon", None),
        ),
        out_specs=(P("lat", "lon", None), P("lat", "lon", None), P(("lon", "lat"))),
        check_vma=False,
    )
```
